32 devices in a mesh: dp: 4 (over y, core), seq: 8 (over z, x).
Axes of the slice: x: 2, y: 2, z: 4, core: 2. Of those that a mesh axis runs over, the one named last changes fastest.
Arguments:
- inputs: bfloat16 [4096, 768], P(('dp', 'seq')), may hold values from -6 to 6
- norm_gain: float32 [768], replicated, may hold values from 0.5 to 1.5
- in_proj: bfloat16 [768, 3352], P(('dp', 'seq')), may hold values from -0.21875 to 0.21875
- conv_weight: float32 [1792, 4], replicated, may hold values from -0.5 to 0.5
- conv_bias: float32 [1792], replicated, may hold values from -0.5 to 0.5
- dt_bias: float32 [24], replicated, may hold values from -10 to -3
- a_log: float32 [24], replicated, may hold values from -1 to 1.5
- skip_gain: float32 [24], replicated, may hold values from 0.5 to 1.5
- gated_gain: float32 [1536], replicated, may hold values from 0.5 to 1.5
- out_proj: bfloat16 [768, 1536], P(('dp', 'seq')), may hold values from -0.15625 to 0.15625
- cotangent: bfloat16 [4096, 768], P(('dp', 'seq')), may hold values from -6 to 6
Outputs:
- layer_out: bfloat16 [4096, 768], P(('dp', 'seq'))
- input_grad: float32 [4096, 768], P(('dp', 'seq'))
- in_proj_grad: float32 [768, 3352], P(('dp', 'seq'))
- out_proj_grad: float32 [768, 1536], P(('dp', 'seq'))
- norm_gain_grad: float32 [768], replicated
- conv_weight_grad: float32 [1792, 4], replicated
- conv_bias_grad: float32 [1792], replicated
- dt_bias_grad: float32 [24], replicated
- a_log_grad: float32 [24], replicated
- skip_grad: float32 [24], replicated
- gated_gain_grad: float32 [1536], replicated
The draws below stay inside these ranges and needn't reach their ends.
All inputs are finite; a program needn't handle non-finite values.
Results may differ from the reference program's by a relative error of at most 0.015.
Values may be sent and summed in bfloat16 or wider, within the bound.
A program may use at most 192 MiB of HBM per device.

```python
import jax
import jax.numpy as jnp
from jax import lax

D = 768
HEADS = 24
HEAD_DIM = 64
STATE = 128
CONV = 4
SPAN = 256
TOK_DEV = 128
DI = 1536
XBC = 1792
PROJ = 3352
LENGTH = 1024
TOKENS = 4096
N_DP = 4
N_SEQ = 8


def raised(array, key, source, target, shards_of, factor):
    owner, partner = [(jnp.arange(array.shape[dim]) // (array.shape[dim] // shards_of)).reshape([-1 if axis == dim else 1 for axis in range(array.ndim)]) for dim in (source, target)]
    chosen = jax.random.permutation(key, shards_of)[partner]
    strong = (owner == chosen) | (owner == (partner + shards_of // 2) % shards_of)
    return jnp.where(strong, factor * array, array)


def block_scale(stream_key, dims, cuts, smallest, top_value):
    level, own = 1.0, jax.random.fold_in(stream_key, 6)
    for axis_at, blocks in cuts:
        steps = jnp.exp(jax.random.uniform(jax.random.fold_in(own, axis_at), (blocks,), jnp.float32, smallest / len(cuts), top_value / len(cuts)))
        level = level * jnp.repeat(steps, dims[axis_at] // blocks).reshape([-1 if axis == axis_at else 1 for axis in range(len(dims))])
    return level


def bell_draw(key, dims, width, most, split=(), dtype=jnp.bfloat16):
    array = width * jax.random.normal(key, dims, jnp.float32)
    if split:
        array = array * block_scale(key, dims, split, -0.22, 0.18)
    return jnp.clip(array, -most, most).astype(dtype)


def gaussian_with(rng, shape, scale, bound, shards, heavy, held_as=jnp.bfloat16):
    entries = scale * jax.random.normal(rng, shape, jnp.float32)
    if shards:
        entries = entries * block_scale(rng, shape, shards, -0.22, 0.18)
    return jnp.clip(raised(entries, jax.random.fold_in(rng, 3), *heavy), -bound, bound).astype(held_as)


def setup_inputs(seed: int = 0) -> dict:
    splits = jax.random.split(jax.random.key(seed), 12)
    return {
        "inputs": bell_draw(splits[0], (TOKENS, D), 1.0, 6.0, ((0, 32),)),
        "norm_gain": jnp.clip(1.0 + 0.1 * jax.random.normal(splits[1], (D,), jnp.float32), 0.5, 1.5),
        "in_proj": bell_draw(splits[2], (D, PROJ), D ** -0.5, 0.21875, ((0, 32),)),
        "conv_weight": jnp.clip(jax.random.uniform(splits[3], (XBC, CONV), jnp.float32, -0.5, 0.5), -0.5, 0.5),
        "conv_bias": jnp.clip(jax.random.uniform(splits[4], (XBC,), jnp.float32, -0.5, 0.5), -0.5, 0.5),
        "dt_bias": jnp.clip(jax.random.uniform(splits[5], (HEADS,), jnp.float32, -10.0, -3.0), -10.0, -3.0),
        "a_log": jnp.clip(jax.random.uniform(splits[6], (HEADS,), jnp.float32, -1.0, 1.5), -1.0, 1.5),
        "skip_gain": jnp.clip(jax.random.uniform(splits[7], (HEADS,), jnp.float32, 0.5, 1.5), 0.5, 1.5),
        "gated_gain": jnp.clip(1.0 + 0.1 * jax.random.normal(splits[8], (DI,), jnp.float32), 0.5, 1.5),
        "out_proj": bell_draw(splits[9], (D, DI), DI ** -0.5, 0.15625, ((0, 32),)),
        "cotangent": gaussian_with(splits[10], (TOKENS, D), 1.0, 6.0, ((0, 32),), (0, 1, 32, 2.75)),
    }


EPS = 1e-05
HIGH = lax.Precision.HIGHEST

def pre_norm(residual_in, norm_gain):
    scale_rms = lax.rsqrt(lax.optimization_barrier(jnp.mean(residual_in * residual_in, axis=-1, keepdims=True)) + EPS)
    return residual_in * scale_rms * norm_gain

def conv_silu(padded, conv_weight, conv_bias, row_count):
    total = jnp.zeros((row_count, padded.shape[1]), jnp.float32) + conv_bias[None, :]
    for offset in range(conv_weight.shape[1]):
        total = total + conv_weight[:, offset][None, :] * padded[offset:offset + row_count]
    return jax.nn.silu(total)

def ssd_block(heads_x, b_block, c_block, step_block, decay_block, carried):
    cumulative = jnp.cumsum(decay_block, axis=0)
    by_head = cumulative.T
    spread = by_head[:, :, None] - by_head[:, None, :]
    places = jnp.arange(decay_block.shape[0])
    lower = places[:, None] >= places[None, :]
    weights_mat = jnp.exp(jnp.where(lower[None], spread, -jnp.inf))
    intersection = jnp.dot(c_block, b_block.T, precision=HIGH)
    scaled_x = heads_x * step_block[:, :, None]
    scores = weights_mat * intersection[None]
    output = jnp.einsum('hts,shp->thp', scores, scaled_x, precision=HIGH)
    output = output + jnp.einsum('tn,hpn->thp', c_block, carried, precision=HIGH) * jnp.exp(cumulative)[:, :, None]
    tail = jnp.exp(cumulative[-1][None, :] - cumulative)
    fresh = jnp.einsum('shp,sn->hpn', scaled_x * tail[:, :, None], b_block, precision=HIGH)
    return (output, fresh + jnp.exp(cumulative[-1])[:, None, None] * carried)

def ssd_scan(xs, b_mat, c_mat, step, log_decay, block_rows):
    row_count = xs.shape[0]
    count = row_count // block_rows
    pieces = (xs.reshape(count, block_rows, HEADS, HEAD_DIM), b_mat.reshape(count, block_rows, STATE), c_mat.reshape(count, block_rows, STATE), step.reshape(count, block_rows, HEADS), log_decay.reshape(count, block_rows, HEADS))
    start_state = jnp.zeros((HEADS, HEAD_DIM, STATE), jnp.float32)

    def advance(carried, piece):
        output, carried = ssd_block(piece[0], piece[1], piece[2], piece[3], piece[4], carried)
        return (carried, output)
    final, outputs = lax.scan(advance, start_state, pieces)
    return (outputs.reshape(row_count, HEADS * HEAD_DIM), final)

def mid_local(xbc, dt_raw, edge, conv_weight, conv_bias, dt_bias, a_log, block_rows):
    row_count = xbc.shape[0]
    activated = conv_silu(jnp.concatenate([edge, xbc], axis=0), conv_weight, conv_bias, row_count)
    xs = activated[:, :DI]
    b_mat = activated[:, DI:DI + STATE]
    c_mat = activated[:, DI + STATE:]
    step = jax.nn.softplus(dt_raw + dt_bias)
    log_decay = step * -jnp.exp(a_log)
    ssd_out, final = ssd_scan(xs, b_mat, c_mat, step, log_decay, block_rows)
    return (ssd_out, xs, c_mat, jnp.cumsum(log_decay, axis=0), final)

def post_gate(ssd_out, xs, gate_part, skip_gain, gated_gain):
    row_count = xs.shape[0]
    skipped = (xs.reshape(row_count, HEADS, HEAD_DIM) * skip_gain[None, :, None]).reshape(row_count, DI)
    mixed_in = (ssd_out + skipped) * jax.nn.silu(gate_part)
    scale_rms = lax.rsqrt(lax.optimization_barrier(jnp.mean(mixed_in * mixed_in, axis=-1, keepdims=True)) + EPS)
    return mixed_in * scale_rms * gated_gain

def mixer(projected, conv_weight, conv_bias, dt_bias, a_log, skip_gain, gated_gain):
    gate_part = projected[:, :DI]
    xbc = projected[:, DI:DI + XBC]
    dt_raw = projected[:, DI + XBC:]
    edge = jnp.zeros((CONV - 1, XBC), jnp.float32)
    block_rows = SPAN if TOK_DEV % SPAN == 0 else TOK_DEV
    ssd_out, xs, c_mat, cumulative, final = mid_local(xbc, dt_raw, edge, conv_weight, conv_bias, dt_bias, a_log, block_rows)
    return post_gate(ssd_out, xs, gate_part, skip_gain, gated_gain)

def rounded(value):
    return lax.optimization_barrier(value.astype(jnp.bfloat16)).astype(jnp.float32)

def block_grads(normed, projected_cot, cot_rows, gated):
    pieces = (normed.reshape(N_SEQ, TOK_DEV, D), projected_cot.reshape(N_SEQ, TOK_DEV, PROJ), cot_rows.reshape(N_SEQ, TOK_DEV, D), gated.reshape(N_SEQ, TOK_DEV, DI))

    def add_block(totals, piece):
        in_term = jnp.dot(piece[0].T, piece[1], preferred_element_type=jnp.float32)
        out_term = jnp.dot(piece[2].T, piece[3], preferred_element_type=jnp.float32)
        return ((totals[0] + rounded(in_term), totals[1] + rounded(out_term)), None)
    start = (jnp.zeros((D, PROJ), jnp.float32), jnp.zeros((D, DI), jnp.float32))
    totals, unused = lax.scan(add_block, start, pieces)
    return totals

def reference(inputs, norm_gain, in_proj, conv_weight, conv_bias, dt_bias, a_log, skip_gain, gated_gain, out_proj, cotangent):

    def one_sequence(totals, pieces):
        tokens, cot_rows = pieces
        residual_in = tokens.astype(jnp.float32)
        normed_full, norm_back = jax.vjp(pre_norm, residual_in, norm_gain)
        normed = normed_full.astype(jnp.bfloat16)
        projected = jnp.dot(normed, in_proj, preferred_element_type=jnp.float32)
        gated_full, mixer_back = jax.vjp(mixer, projected, conv_weight, conv_bias, dt_bias, a_log, skip_gain, gated_gain)
        gated = gated_full.astype(jnp.bfloat16)
        mixed = jnp.dot(gated, out_proj.T, preferred_element_type=jnp.float32)
        layer_out = (residual_in + mixed).astype(jnp.bfloat16)
        gated_cot = jnp.dot(cot_rows, out_proj, preferred_element_type=jnp.float32)
        grads = mixer_back(gated_cot)
        projected_cot = grads[0].astype(jnp.bfloat16)
        in_grad, out_grad = block_grads(normed, projected_cot, cot_rows, gated)
        normed_cot = jnp.dot(projected_cot, in_proj.T, preferred_element_type=jnp.float32)
        input_part, gain_grad = norm_back(normed_cot)
        input_grad = cot_rows.astype(jnp.float32) + input_part
        updates = (in_grad, out_grad, gain_grad) + tuple(grads[1:])
        totals = tuple((earlier + later for earlier, later in zip(totals, updates)))
        return (totals, (layer_out, input_grad))
    start = (jnp.zeros((D, PROJ), jnp.float32), jnp.zeros((D, DI), jnp.float32), jnp.zeros((D,), jnp.float32), jnp.zeros((XBC, CONV), jnp.float32), jnp.zeros((XBC,), jnp.float32), jnp.zeros((HEADS,), jnp.float32), jnp.zeros((HEADS,), jnp.float32), jnp.zeros((HEADS,), jnp.float32), jnp.zeros((DI,), jnp.float32))
    sequences = (inputs.reshape(N_DP, LENGTH, D), cotangent.reshape(N_DP, LENGTH, D))
    totals, stacked = lax.scan(one_sequence, start, sequences)
    return (stacked[0].reshape(TOKENS, D), stacked[1].reshape(TOKENS, D), totals[0], totals[1], totals[2], totals[3], totals[4], totals[5], totals[6], totals[7], totals[8])
```

```python
from functools import partial

import jax
import jax.numpy as jnp
from jax import lax
from jax.experimental import pallas as pl
from jax.experimental.pallas import tpu as pltpu
from jax.sharding import PartitionSpec as P

HEADS = 24
HEAD_DIM = 64
STATE = 128
CONV = 4
DI = 1536
XBC = 1792
PROJ = DI + XBC + HEADS
LANES = 128
WIDE = -(-PROJ // LANES) * LANES


EPS = 1e-05
HIGH = lax.Precision.HIGHEST
MESH = pl.DeviceIdType.MESH
VMEM_BYTES = 60 * 1024 * 1024


def bits_of(count):
    return count.bit_length() - 1


def bit_at(place, bit):
    return (place // 2**bit) % 2


def places():
    return lax.axis_index("dp"), lax.axis_index("seq")


def partner(bit, seq_bits):
    dp_at, seq_at = places()
    if bit < seq_bits:
        return dp_at, seq_at + (1 - 2 * bit_at(seq_at, bit)) * 2**bit
    up = bit - seq_bits
    return dp_at + (1 - 2 * bit_at(dp_at, up)) * 2**up, seq_at


def greet(bits, seq_bits):
    barrier = pltpu.get_barrier_semaphore()
    for bit in range(bits):
        pl.semaphore_signal(barrier, inc=1, device_id=partner(bit, seq_bits), device_id_type=MESH)
    pl.semaphore_wait(barrier, bits)


def gather_orders(seq_bits, dp_bits):
    x_count = seq_bits // 2
    x_bits = list(range(x_count))
    z_bits = list(range(x_count, seq_bits))[::-1]
    core = [seq_bits]
    y_bits = [seq_bits + 1 + i for i in range(dp_bits - 1)]
    return (
        z_bits + x_bits + y_bits + core,
        z_bits + y_bits + x_bits + core,
        x_bits + z_bits[:1] + y_bits + z_bits[1:] + core,
        y_bits + z_bits[:1] + x_bits + z_bits[1:] + core,
    )


def split_lanes(width, count):
    tiles = width // LANES
    edges = [tiles * i // count * LANES for i in range(count + 1)]
    return [(low, high - low) for low, high in zip(edges, edges[1:])]


def gather_kernel(seq_bits, streams, bits, *refs):
    array_count = 1 + max(stream[0] for stream in streams)
    shards, outs = refs[:array_count], refs[array_count : 2 * array_count]
    send_sem, recv_sem, own_sem = refs[2 * array_count :]
    dp_at, seq_at = places()
    place = dp_at * 2**seq_bits + seq_at
    own = [
        pltpu.make_async_copy(shard, out.at[place], own_sem.at[i])
        for i, (shard, out) in enumerate(zip(shards, outs))
    ]
    for copy in own:
        copy.start()
    greet(bits, seq_bits)
    for copy in own:
        copy.wait()

    def landed(stream, stage, sem):
        which, low, width, _ = streams[stream]
        view = outs[which].at[pl.ds(0, 2**stage), :, pl.ds(low, width)]
        pltpu.make_async_copy(view, view, sem.at[stream, stage]).wait()

    for stage in range(bits + 1):
        for stream, (which, low, width, order) in enumerate(streams):
            if stage > 0:
                landed(stream, stage - 1, recv_sem)
            if stage == bits:
                continue
            free = order[:stage]
            run = 0
            while run in free:
                run += 1
            base = place
            for bit in free:
                base = base - bit_at(place, bit) * 2**bit
            upper = [bit for bit in free if bit > run]
            for combo in range(2 ** len(upper)):
                start = base + sum(2**bit for i, bit in enumerate(upper) if combo >> i & 1)
                view = outs[which].at[pl.ds(start, 2**run), :, pl.ds(low, width)]
                pltpu.make_async_remote_copy(
                    src_ref=view,
                    dst_ref=view,
                    send_sem=send_sem.at[stream, stage],
                    recv_sem=recv_sem.at[stream, stage],
                    device_id=partner(order[stage], seq_bits),
                    device_id_type=MESH,
                ).start()
    for stage in range(bits):
        for stream in range(len(streams)):
            landed(stream, stage, send_sem)


def gather_all(shards, collective_id):
    seq_bits, dp_bits = bits_of(lax.axis_size("seq")), bits_of(lax.axis_size("dp"))
    bits = seq_bits + dp_bits
    orders = gather_orders(seq_bits, dp_bits)
    streams = [
        (which, low, width, order)
        for which, shard in enumerate(shards)
        for (low, width), order in zip(split_lanes(shard.shape[1], len(orders)), orders)
    ]
    return pl.pallas_call(
        partial(gather_kernel, seq_bits, streams, bits),
        out_shape=[jax.ShapeDtypeStruct((2**bits, *a.shape), a.dtype) for a in shards],
        in_specs=[pl.BlockSpec(memory_space=pltpu.VMEM)] * len(shards),
        out_specs=[pl.BlockSpec(memory_space=pl.ANY)] * len(shards),
        scratch_shapes=[
            pltpu.SemaphoreType.DMA((len(streams), bits)),
            pltpu.SemaphoreType.DMA((len(streams), bits)),
            pltpu.SemaphoreType.DMA((len(shards),)),
        ],
        compiler_params=pltpu.CompilerParams(
            collective_id=collective_id, has_side_effects=True, vmem_limit_bytes=VMEM_BYTES
        ),
        name="gather_rows",
    )(*shards)


def sum_kernel(seq_bits, streams, bits, array_count, *refs):
    terms, vector = refs[:array_count], refs[array_count]
    outs, vector_out = refs[array_count + 1 : 2 * array_count + 1], refs[2 * array_count + 1]
    held = refs[2 * array_count + 2 : 2 * array_count + 2 + len(streams) * bits]
    rest = refs[2 * array_count + 2 + len(streams) * bits :]
    vector_in, vector_sum, send_sem, recv_sem, vector_send, vector_recv = rest
    dp_at, seq_at = places()
    place = dp_at * 2**seq_bits + seq_at
    greet(bits, seq_bits)

    def source(stream, stage):
        which, low, width, _ = streams[stream]
        if stage == 0:
            return terms[which], pl.ds(low, width)
        return held[stream * bits + stage - 1], pl.ds(0, width)

    def position(stream, stage):
        order = streams[stream][3]
        remaining = sorted(order[stage:])
        return remaining.index(order[stage]), bit_at(place, order[stage])

    def landed(stream, stage, sem):
        view = held[stream * bits + stage]
        pltpu.make_async_copy(view, view, sem.at[stream, stage]).wait()

    def vector_copy(stage):
        return pltpu.make_async_remote_copy(
            src_ref=vector if stage == 0 else vector_sum.at[stage - 1],
            dst_ref=vector_in.at[stage],
            send_sem=vector_send.at[stage],
            recv_sem=vector_recv.at[stage],
            device_id=partner(stage, seq_bits),
            device_id_type=MESH,
        )

    for stage in range(bits + 1):
        if stage > 0:
            vector_copy(stage - 1).wait_recv()
            before = vector[...] if stage == 1 else vector_sum[stage - 2]
            total = before + vector_in[stage - 1]
            if stage < bits:
                vector_sum[stage - 1] = total
            else:
                vector_out[...] = total
        if stage < bits:
            vector_copy(stage).start()
        for stream, (which, low, width, order) in enumerate(streams):
            if stage > 0:
                landed(stream, stage - 1, recv_sem)
                spot, mine = position(stream, stage - 1)
                kept, lanes = source(stream, stage - 1)
                came = held[stream * bits + stage - 1]
                if stage == bits:
                    outs[which][:, pl.ds(low, width)] = kept[mine, :, lanes].astype(
                        jnp.float32
                    ) + came[0].astype(jnp.float32)
                    continue

                def add_one(block, carry, spot=spot, mine=mine, kept=kept, lanes=lanes, came=came):
                    from_block = (block // 2**spot) * 2 ** (spot + 1) + mine * 2**spot
                    from_block = from_block + block % 2**spot
                    added = kept[from_block, :, lanes].astype(jnp.float32) + came[block].astype(
                        jnp.float32
                    )
                    came[block] = added.astype(came.dtype)
                    return carry

                lax.fori_loop(0, 2 ** (bits - stage), add_one, 0)
            spot, mine = position(stream, stage)
            sent, lanes = source(stream, stage)
            for high in range(2 ** (bits - stage - 1 - spot)):
                start = high * 2 ** (spot + 1) + (1 - mine) * 2**spot
                pltpu.make_async_remote_copy(
                    src_ref=sent.at[pl.ds(start, 2**spot), :, lanes],
                    dst_ref=held[stream * bits + stage].at[pl.ds(high * 2**spot, 2**spot)],
                    send_sem=send_sem.at[stream, stage],
                    recv_sem=recv_sem.at[stream, stage],
                    device_id=partner(order[stage], seq_bits),
                    device_id_type=MESH,
                ).start()
    for stage in range(bits):
        vector_copy(stage).wait_send()
        for stream in range(len(streams)):
            landed(stream, stage, send_sem)


def sum_to_owners(terms, vector, collective_id):
    seq_bits, dp_bits = bits_of(lax.axis_size("seq")), bits_of(lax.axis_size("dp"))
    bits = seq_bits + dp_bits
    orders = [order[::-1] for order in gather_orders(seq_bits, dp_bits)]
    terms = [term.reshape(2**bits, -1, term.shape[1]) for term in terms]
    streams = [
        (which, low, width, order)
        for which, term in enumerate(terms)
        for (low, width), order in zip(split_lanes(term.shape[2], len(orders)), orders)
    ]
    rows = terms[0].shape[1]
    in_vmem = pl.BlockSpec(memory_space=pltpu.VMEM)
    held = [
        pltpu.VMEM((2 ** (bits - 1 - stage), rows, width), jnp.bfloat16)
        for _, _, width, _ in streams
        for stage in range(bits)
    ]
    return pl.pallas_call(
        partial(sum_kernel, seq_bits, streams, bits, len(terms)),
        out_shape=[jax.ShapeDtypeStruct(a.shape[1:], jnp.float32) for a in terms]
        + [jax.ShapeDtypeStruct(vector.shape, vector.dtype)],
        in_specs=[in_vmem] * (len(terms) + 1),
        out_specs=[in_vmem] * (len(terms) + 1),
        scratch_shapes=held
        + [
            pltpu.VMEM((bits, *vector.shape), jnp.float32),
            pltpu.VMEM((bits, *vector.shape), jnp.float32),
            pltpu.SemaphoreType.DMA((len(streams), bits)),
            pltpu.SemaphoreType.DMA((len(streams), bits)),
            pltpu.SemaphoreType.DMA((bits,)),
            pltpu.SemaphoreType.DMA((bits,)),
        ],
        compiler_params=pltpu.CompilerParams(
            collective_id=collective_id, has_side_effects=True, vmem_limit_bytes=VMEM_BYTES
        ),
        name="sum_rows",
    )(*terms, vector)


def scan_kernel(count, reverse, state, decay, out, came, came_decay, ready, *sems):
    out_send, out_recv, decay_send, decay_recv, back_send, back_recv = sems
    dp_at, seq_at = places()
    barrier = pltpu.get_barrier_semaphore()
    peers = [(seq_at + hop) % count for hop in range(1, count)]
    for peer in peers:
        pl.semaphore_signal(barrier, inc=1, device_id=(dp_at, peer), device_id_type=MESH)
    pl.semaphore_wait(barrier, count - 1)

    def copy(hop, which):
        target = (seq_at + hop) % count
        source, landing, send_sem, recv_sem = (
            (state.at[target], came.at[seq_at], out_send, out_recv),
            (decay, came_decay.at[seq_at], decay_send, decay_recv),
            (ready.at[target], out.at[seq_at], back_send, back_recv),
        )[which]
        return pltpu.make_async_remote_copy(
            src_ref=source,
            dst_ref=landing,
            send_sem=send_sem.at[hop],
            recv_sem=recv_sem.at[hop],
            device_id=(dp_at, target),
            device_id_type=MESH,
        )

    for hop in range(1, count):
        copy(hop, 0).start()
        copy(hop, 1).start()
    came[seq_at] = state[seq_at]
    came_decay[seq_at] = decay[...]
    for hop in range(1, count):
        copy(hop, 0).wait_recv()
        copy(hop, 1).wait_recv()
    total = jnp.zeros(state.shape[1:], jnp.float32)
    for place in range(count)[:: -1 if reverse else 1]:
        ready[place] = total.astype(ready.dtype)
        total = came_decay[place] * total + came[place].astype(jnp.float32)
    for hop in range(1, count):
        copy(hop, 2).start()
    out[seq_at] = ready[seq_at]
    for hop in range(1, count):
        copy(hop, 2).wait_recv()
    for hop in range(1, count):
        for which in range(3):
            copy(hop, which).wait_send()


def scan_states(state, decay, reverse, collective_id):
    count = lax.axis_size("seq")
    state = state.astype(jnp.bfloat16).reshape(count, STATE // count, DI)
    in_vmem = pl.BlockSpec(memory_space=pltpu.VMEM)
    sems = [pltpu.SemaphoreType.DMA((count,))] * 6
    got = pl.pallas_call(
        partial(scan_kernel, count, reverse),
        out_shape=jax.ShapeDtypeStruct(state.shape, state.dtype),
        in_specs=[in_vmem, in_vmem],
        out_specs=in_vmem,
        scratch_shapes=[
            pltpu.VMEM(state.shape, state.dtype),
            pltpu.VMEM((count, 1, DI), jnp.float32),
            pltpu.VMEM(state.shape, state.dtype),
        ]
        + sems,
        compiler_params=pltpu.CompilerParams(
            collective_id=collective_id, has_side_effects=True, vmem_limit_bytes=VMEM_BYTES
        ),
        name="scan_back" if reverse else "scan_states",
    )(state, decay[None, :])
    return got.reshape(STATE, DI).astype(jnp.float32)


def passed_along(value, axis, steps):
    count = lax.axis_size(axis)
    first, last = (max(0, -steps), min(count, count - steps))
    return lax.ppermute(value, axis, [(source, source + steps) for source in range(first, last)])


def pre_norm(residual_in, norm_gain):
    scale_rms = lax.rsqrt(jnp.mean(residual_in * residual_in, axis=-1, keepdims=True) + EPS)
    return residual_in * scale_rms * norm_gain


def conv_silu(padded, conv_weight, conv_bias, row_count):
    total = jnp.zeros((row_count, padded.shape[1]), jnp.float32) + conv_bias[None, :]
    for offset in range(conv_weight.shape[1]):
        total = total + conv_weight[:, offset][None, :] * padded[offset : offset + row_count]
    return jax.nn.silu(total)


def spread_heads(by_head):
    return jnp.repeat(by_head, HEAD_DIM, axis=-1)


def ssd_block(xs, b_block, c_block, step_block, decay_block):
    row_count = xs.shape[0]
    at = jnp.arange(row_count)
    lower = at[:, None] >= at[None, :]
    cumulative = jnp.dot(lower.astype(jnp.float32), decay_block, precision=HIGH)
    by_head = cumulative.T
    spread = by_head[:, :, None] - by_head[:, None, :]
    weights_mat = jnp.exp(jnp.where(lower[None], spread, -jnp.inf))
    intersection = jnp.dot(c_block, b_block.T, precision=HIGH)
    scaled_x = xs * spread_heads(step_block)
    scores = weights_mat * intersection[None]
    output = jnp.einsum(
        "hts,shp->thp", scores, scaled_x.reshape(row_count, HEADS, HEAD_DIM), precision=HIGH
    )
    tail = jnp.exp(cumulative[-1][None, :] - cumulative)
    fresh = jnp.dot(b_block.T, scaled_x * spread_heads(tail), precision=HIGH)
    return output.reshape(row_count, DI), cumulative, fresh


def mid_local(xbc, dt_raw, edge, conv_weight, conv_bias, dt_bias, a_log):
    row_count = xbc.shape[0]
    activated = conv_silu(jnp.concatenate([edge, xbc], axis=0), conv_weight, conv_bias, row_count)
    xs = activated[:, :DI]
    b_mat = activated[:, DI : DI + STATE]
    c_mat = activated[:, DI + STATE :]
    step = jax.nn.softplus(dt_raw + dt_bias)
    log_decay = step * -jnp.exp(a_log)
    ssd_out, cumulative, final = ssd_block(xs, b_mat, c_mat, step, log_decay)
    return (ssd_out, xs, c_mat, cumulative, final)


def post_gate(ssd_out, xs, gate_part, skip_gain, gated_gain):
    row_count = xs.shape[0]
    skipped = (xs.reshape(row_count, HEADS, HEAD_DIM) * skip_gain[None, :, None]).reshape(
        row_count, DI
    )
    mixed_in = (ssd_out + skipped) * jax.nn.silu(gate_part)
    scale_rms = lax.rsqrt(jnp.mean(mixed_in * mixed_in, axis=-1, keepdims=True) + EPS)
    return mixed_in * scale_rms * gated_gain


def contract_rows(left, right):
    return lax.dot_general(
        left, right, (((0,), (0,)), ((), ())), preferred_element_type=jnp.float32
    )


def contract_cols(left, right):
    return lax.dot_general(
        left, right, (((1,), (1,)), ((), ())), preferred_element_type=jnp.float32
    )


def body(
    inputs,
    norm_gain,
    in_proj,
    conv_weight,
    conv_bias,
    dt_bias,
    a_log,
    skip_gain,
    gated_gain,
    out_proj,
    cotangent,
):
    row_count = inputs.shape[0]
    residual_in = inputs.astype(jnp.float32)
    normed_full, norm_back = jax.vjp(pre_norm, residual_in, norm_gain)
    normed = normed_full.astype(jnp.bfloat16)
    in_whole, out_whole = gather_all(
        [jnp.pad(in_proj, ((0, 0), (0, WIDE - PROJ))), out_proj], collective_id=1
    )
    in_whole = in_whole.reshape(-1, WIDE)
    out_whole = out_whole.reshape(-1, DI)
    projected = jnp.dot(normed, in_whole, preferred_element_type=jnp.float32)
    gate_part = projected[:, :DI]
    xbc = projected[:, DI : DI + XBC]
    dt_raw = projected[:, DI + XBC : PROJ]
    edge = passed_along(xbc[row_count - (CONV - 1) :], "seq", 1)
    primal, mid_back = jax.vjp(
        mid_local, xbc, dt_raw, edge, conv_weight, conv_bias, dt_bias, a_log
    )
    local_out, xs, c_mat, cumulative, s_local = primal
    decay = jnp.exp(cumulative[-1])
    wide_decay = spread_heads(decay)
    state_in = scan_states(s_local, wide_decay, False, collective_id=2)
    weighted = spread_heads(jnp.exp(cumulative))
    carried_part = jnp.dot(c_mat, state_in, precision=HIGH) * weighted
    ssd_out = local_out + carried_part
    gated_full, post_back = jax.vjp(post_gate, ssd_out, xs, gate_part, skip_gain, gated_gain)
    gated = gated_full.astype(jnp.bfloat16)
    mixed = contract_cols(gated, out_whole)
    layer_out = (residual_in + mixed).astype(jnp.bfloat16)
    gated_cot = jnp.dot(cotangent, out_whole, preferred_element_type=jnp.float32)
    ssd_cot, xs_cot, gate_cot, skip_grad, gated_gain_grad = post_back(gated_cot)
    scaled_cot = ssd_cot * weighted
    local_grad = jnp.dot(c_mat.T, scaled_cot, precision=HIGH)
    later_grad = scan_states(local_grad, wide_decay, True, collective_id=3)
    c_cot = lax.dot_general(scaled_cot, state_in, (((1,), (1,)), ((), ())), precision=HIGH)
    cum_cot = jnp.sum((ssd_cot * carried_part).reshape(row_count, HEADS, HEAD_DIM), axis=2)
    last_cot = jnp.sum(later_grad * state_in, axis=0).reshape(HEADS, HEAD_DIM).sum(axis=1) * decay
    is_last = (jnp.arange(row_count) == row_count - 1)[:, None]
    cum_cot = cum_cot + jnp.where(is_last, last_cot[None, :], 0.0)
    mid_grads = mid_back((ssd_cot, xs_cot, c_cot, cum_cot, later_grad))
    xbc_cot, dt_cot, edge_cot, conv_weight_grad, conv_bias_grad, dt_bias_grad, a_log_grad = (
        mid_grads
    )
    edge_back = passed_along(edge_cot, "seq", -1)
    xbc_cot = xbc_cot + jnp.pad(edge_back, ((row_count - (CONV - 1), 0), (0, 0)))
    projected_cot = jnp.concatenate(
        [gate_cot, xbc_cot, dt_cot, jnp.zeros((row_count, WIDE - PROJ), jnp.float32)], axis=1
    ).astype(jnp.bfloat16)
    in_term = contract_rows(normed, projected_cot).astype(jnp.bfloat16)
    out_term = contract_rows(cotangent, gated).astype(jnp.bfloat16)
    normed_cot = contract_cols(projected_cot, in_whole)
    input_part, norm_gain_grad = norm_back(normed_cot)
    input_grad = cotangent.astype(jnp.float32) + input_part
    small = (
        norm_gain_grad,
        conv_weight_grad.T,
        conv_bias_grad,
        gated_gain_grad,
        dt_bias_grad,
        a_log_grad,
        skip_grad,
    )
    flat = jnp.concatenate([a.reshape(-1) for a in small])
    tile = 8 * LANES
    flat = jnp.pad(flat, (0, -flat.shape[0] % tile))
    in_proj_grad, out_proj_grad, summed = sum_to_owners(
        [in_term, out_term], flat.reshape(-1, LANES), collective_id=4
    )
    summed = summed.reshape(-1)
    parts, at = [], 0
    for a in small:
        parts.append(summed[at : at + a.size].reshape(a.shape))
        at += a.size
    return (
        layer_out,
        input_grad,
        in_proj_grad[:, :PROJ],
        out_proj_grad,
        parts[0],
        parts[1].T,
        parts[2],
        parts[4],
        parts[5],
        parts[6],
        parts[3],
    )


def solution(mesh):
    placed = (
        P(("dp", "seq"), None),
        P(),
        P(("dp", "seq"), None),
        P(),
        P(),
        P(),
        P(),
        P(),
        P(),
        P(("dp", "seq"), None),
        P(("dp", "seq"), None),
    )
    return jax.shard_map(
        body,
        mesh=mesh,
        in_specs=placed,
        out_specs=(
            P(("dp", "seq"), None),
            P(("dp", "seq"), None),
            P(("dp", "seq"), None),
            P(("dp", "seq"), None),
            P(),
            P(),
            P(),
            P(),
            P(),
            P(),
            P(),
        ),
        check_vma=False,
    )
```

```python
from functools import partial

import jax
import jax.numpy as jnp
from jax import lax
from jax.experimental import pallas as pl
from jax.experimental.pallas import tpu as pltpu
from jax.sharding import PartitionSpec as P

HEADS = 24
HEAD_DIM = 64
STATE = 128
CONV = 4
DI = 1536
XBC = 1792
PROJ = DI + XBC + HEADS
LANES = 128
WIDE = -(-PROJ // LANES) * LANES


EPS = 1e-05
HIGH = lax.Precision.HIGHEST
MESH = pl.DeviceIdType.MESH
VMEM_BYTES = 60 * 1024 * 1024


def bits_of(count):
    return count.bit_length() - 1


def bit_at(place, bit):
    return (place // 2**bit) % 2


def places():
    return lax.axis_index("dp"), lax.axis_index("seq")


def partner(bit, seq_bits):
    dp_at, seq_at = places()
    if bit < seq_bits:
        return dp_at, seq_at + (1 - 2 * bit_at(seq_at, bit)) * 2**bit
    up = bit - seq_bits
    return dp_at + (1 - 2 * bit_at(dp_at, up)) * 2**up, seq_at


def greet(bits, seq_bits):
    barrier = pltpu.get_barrier_semaphore()
    for bit in range(bits):
        pl.semaphore_signal(barrier, inc=1, device_id=partner(bit, seq_bits), device_id_type=MESH)
    pl.semaphore_wait(barrier, bits)


def gather_orders(seq_bits, dp_bits):
    x_count = seq_bits // 2
    x_bits = list(range(x_count))
    z_bits = list(range(x_count, seq_bits))[::-1]
    core = [seq_bits]
    y_bits = [seq_bits + 1 + i for i in range(dp_bits - 1)]
    return (
        z_bits + x_bits + y_bits + core,
        z_bits + y_bits + x_bits + core,
        x_bits + z_bits[:1] + y_bits + z_bits[1:] + core,
        y_bits + z_bits[:1] + x_bits + z_bits[1:] + core,
    )


def split_lanes(width, count):
    tiles = width // LANES
    edges = [tiles * i // count * LANES for i in range(count + 1)]
    return [(low, high - low) for low, high in zip(edges, edges[1:])]


def gather_kernel(seq_bits, streams, bits, *refs):
    array_count = 1 + max(stream[0] for stream in streams)
    shards, outs = refs[:array_count], refs[array_count : 2 * array_count]
    send_sem, recv_sem, own_sem = refs[2 * array_count :]
    dp_at, seq_at = places()
    place = dp_at * 2**seq_bits + seq_at
    own = [
        pltpu.make_async_copy(shard, out.at[place], own_sem.at[i])
        for i, (shard, out) in enumerate(zip(shards, outs))
    ]
    for copy in own:
        copy.start()
    greet(bits, seq_bits)
    for copy in own:
        copy.wait()

    def landed(stream, stage, sem):
        which, low, width, _ = streams[stream]
        view = outs[which].at[pl.ds(0, 2**stage), :, pl.ds(low, width)]
        pltpu.make_async_copy(view, view, sem.at[stream, stage]).wait()

    for stage in range(bits + 1):
        for stream, (which, low, width, order) in enumerate(streams):
            if stage > 0:
                landed(stream, stage - 1, recv_sem)
            if stage == bits:
                continue
            free = order[:stage]
            run = 0
            while run in free:
                run += 1
            base = place
            for bit in free:
                base = base - bit_at(place, bit) * 2**bit
            upper = [bit for bit in free if bit > run]
            for combo in range(2 ** len(upper)):
                start = base + sum(2**bit for i, bit in enumerate(upper) if combo >> i & 1)
                view = outs[which].at[pl.ds(start, 2**run), :, pl.ds(low, width)]
                pltpu.make_async_remote_copy(
                    src_ref=view,
                    dst_ref=view,
                    send_sem=send_sem.at[stream, stage],
                    recv_sem=recv_sem.at[stream, stage],
                    device_id=partner(order[stage], seq_bits),
                    device_id_type=MESH,
                ).start()
    for stage in range(bits):
        for stream in range(len(streams)):
            landed(stream, stage, send_sem)


def gather_all(shards, collective_id):
    seq_bits, dp_bits = bits_of(lax.axis_size("seq")), bits_of(lax.axis_size("dp"))
    bits = seq_bits + dp_bits
    orders = gather_orders(seq_bits, dp_bits)
    streams = [
        (which, low, width, order)
        for which, shard in enumerate(shards)
        for (low, width), order in zip(split_lanes(shard.shape[1], len(orders)), orders)
    ]
    return pl.pallas_call(
        partial(gather_kernel, seq_bits, streams, bits),
        out_shape=[jax.ShapeDtypeStruct((2**bits, *a.shape), a.dtype) for a in shards],
        in_specs=[pl.BlockSpec(memory_space=pltpu.VMEM)] * len(shards),
        out_specs=[pl.BlockSpec(memory_space=pl.ANY)] * len(shards),
        scratch_shapes=[
            pltpu.SemaphoreType.DMA((len(streams), bits)),
            pltpu.SemaphoreType.DMA((len(streams), bits)),
            pltpu.SemaphoreType.DMA((len(shards),)),
        ],
        compiler_params=pltpu.CompilerParams(
            collective_id=collective_id, has_side_effects=True, vmem_limit_bytes=VMEM_BYTES
        ),
        name="gather_rows",
    )(*shards)


def sum_kernel(seq_bits, streams, bits, array_count, *refs):
    terms, vector = refs[:array_count], refs[array_count]
    outs, vector_out = refs[array_count + 1 : 2 * array_count + 1], refs[2 * array_count + 1]
    held = refs[2 * array_count + 2 : 2 * array_count + 2 + len(streams) * bits]
    rest = refs[2 * array_count + 2 + len(streams) * bits :]
    vector_in, vector_sum, send_sem, recv_sem, vector_send, vector_recv = rest
    dp_at, seq_at = places()
    place = dp_at * 2**seq_bits + seq_at
    greet(bits, seq_bits)

    def source(stream, stage):
        which, low, width, _ = streams[stream]
        if stage == 0:
            return terms[which], pl.ds(low, width)
        return held[stream * bits + stage - 1], pl.ds(0, width)

    def position(stream, stage):
        order = streams[stream][3]
        remaining = sorted(order[stage:])
        return remaining.index(order[stage]), bit_at(place, order[stage])

    def landed(stream, stage, sem):
        view = held[stream * bits + stage]
        pltpu.make_async_copy(view, view, sem.at[stream, stage]).wait()

    def vector_copy(stage):
        return pltpu.make_async_remote_copy(
            src_ref=vector if stage == 0 else vector_sum.at[stage - 1],
            dst_ref=vector_in.at[stage],
            send_sem=vector_send.at[stage],
            recv_sem=vector_recv.at[stage],
            device_id=partner(stage, seq_bits),
            device_id_type=MESH,
        )

    for stage in range(bits + 1):
        if stage > 0:
            vector_copy(stage - 1).wait_recv()
            before = vector[...] if stage == 1 else vector_sum[stage - 2]
            total = before + vector_in[stage - 1]
            if stage < bits:
                vector_sum[stage - 1] = total
            else:
                vector_out[...] = total
        if stage < bits:
            vector_copy(stage).start()
        for stream, (which, low, width, order) in enumerate(streams):
            if stage > 0:
                landed(stream, stage - 1, recv_sem)
                spot, mine = position(stream, stage - 1)
                kept, lanes = source(stream, stage - 1)
                came = held[stream * bits + stage - 1]
                if stage == bits:
                    outs[which][:, pl.ds(low, width)] = kept[mine, :, lanes].astype(
                        jnp.float32
                    ) + came[0].astype(jnp.float32)
                    continue

                def add_one(block, carry, spot=spot, mine=mine, kept=kept, lanes=lanes, came=came):
                    from_block = (block // 2**spot) * 2 ** (spot + 1) + mine * 2**spot
                    from_block = from_block + block % 2**spot
                    added = kept[from_block, :, lanes].astype(jnp.float32) + came[block].astype(
                        jnp.float32
                    )
                    came[block] = added.astype(came.dtype)
                    return carry

                lax.fori_loop(0, 2 ** (bits - stage), add_one, 0)
            spot, mine = position(stream, stage)
            sent, lanes = source(stream, stage)
            for high in range(2 ** (bits - stage - 1 - spot)):
                start = high * 2 ** (spot + 1) + (1 - mine) * 2**spot
                pltpu.make_async_remote_copy(
                    src_ref=sent.at[pl.ds(start, 2**spot), :, lanes],
                    dst_ref=held[stream * bits + stage].at[pl.ds(high * 2**spot, 2**spot)],
                    send_sem=send_sem.at[stream, stage],
                    recv_sem=recv_sem.at[stream, stage],
                    device_id=partner(order[stage], seq_bits),
                    device_id_type=MESH,
                ).start()
    for stage in range(bits):
        vector_copy(stage).wait_send()
        for stream in range(len(streams)):
            landed(stream, stage, send_sem)


def sum_to_owners(terms, vector, collective_id):
    seq_bits, dp_bits = bits_of(lax.axis_size("seq")), bits_of(lax.axis_size("dp"))
    bits = seq_bits + dp_bits
    orders = [order[::-1] for order in gather_orders(seq_bits, dp_bits)]
    terms = [term.reshape(2**bits, -1, term.shape[1]) for term in terms]
    streams = [
        (which, low, width, order)
        for which, term in enumerate(terms)
        for (low, width), order in zip(split_lanes(term.shape[2], len(orders)), orders)
    ]
    rows = terms[0].shape[1]
    in_vmem = pl.BlockSpec(memory_space=pltpu.VMEM)
    held = [
        pltpu.VMEM((2 ** (bits - 1 - stage), rows, width), jnp.bfloat16)
        for _, _, width, _ in streams
        for stage in range(bits)
    ]
    return pl.pallas_call(
        partial(sum_kernel, seq_bits, streams, bits, len(terms)),
        out_shape=[jax.ShapeDtypeStruct(a.shape[1:], jnp.float32) for a in terms]
        + [jax.ShapeDtypeStruct(vector.shape, vector.dtype)],
        in_specs=[in_vmem] * (len(terms) + 1),
        out_specs=[in_vmem] * (len(terms) + 1),
        scratch_shapes=held
        + [
            pltpu.VMEM((bits, *vector.shape), jnp.float32),
            pltpu.VMEM((bits, *vector.shape), jnp.float32),
            pltpu.SemaphoreType.DMA((len(streams), bits)),
            pltpu.SemaphoreType.DMA((len(streams), bits)),
            pltpu.SemaphoreType.DMA((bits,)),
            pltpu.SemaphoreType.DMA((bits,)),
        ],
        compiler_params=pltpu.CompilerParams(
            collective_id=collective_id, has_side_effects=True, vmem_limit_bytes=VMEM_BYTES
        ),
        name="sum_rows",
    )(*terms, vector)


GROUP = 4
GROUP_LANES = GROUP * HEAD_DIM


def inner_product(left, right, dims):
    return lax.dot_general(
        left, right, (dims, ((), ())), precision=HIGH, preferred_element_type=jnp.float32
    )


def group_lanes(group):
    return pl.ds(pl.multiple_of(group * GROUP_LANES, GROUP_LANES), GROUP_LANES)


def head_weights(cumulative, head):
    row = cumulative[pl.ds(head, 1), :]
    count = row.shape[1]
    spread = jnp.broadcast_to(row, (count, count))
    later = lax.broadcasted_iota(jnp.int32, (count, count), 0)
    earlier = lax.broadcasted_iota(jnp.int32, (count, count), 1)
    return jnp.exp(jnp.where(later >= earlier, spread.T - spread, -jnp.inf))


def inside_work(first, last, scaled_x, b_mat, c_mat, cumulative, output, crossed):
    if first == 0:
        crossed[...] = inner_product(c_mat[...], b_mat[...], ((1,), (1,)))

    def one(group, carry):
        values = scaled_x[:, group_lanes(group)]
        parts = []
        for i in range(GROUP):
            scores = head_weights(cumulative, group * GROUP + i) * crossed[...]
            head = values[:, i * HEAD_DIM : (i + 1) * HEAD_DIM]
            parts.append(inner_product(scores, head, ((1,), (0,))))
        output[:, group_lanes(group)] = jnp.concatenate(parts, axis=1)
        return carry

    lax.fori_loop(first, last, one, 0)


def inside_back(
    first,
    last,
    output_cot,
    scaled_x,
    b_mat,
    c_mat,
    cumulative,
    scaled_cot,
    b_cot,
    c_cot,
    cumulative_cot,
    crossed,
    crossed_cot,
):
    if first == 0:
        crossed[...] = inner_product(c_mat[...], b_mat[...], ((1,), (1,)))
        crossed_cot[...] = jnp.zeros_like(crossed_cot)

    def one(group, carry):
        values = scaled_x[:, group_lanes(group)]
        cots = output_cot[:, group_lanes(group)]
        parts = []
        total = crossed_cot[...]
        for i in range(GROUP):
            weights = head_weights(cumulative, group * GROUP + i)
            scores = weights * crossed[...]
            head = values[:, i * HEAD_DIM : (i + 1) * HEAD_DIM]
            cot = cots[:, i * HEAD_DIM : (i + 1) * HEAD_DIM]
            weighted = weights * inner_product(cot, head, ((1,), (1,)))
            total = total + weighted
            parts.append(inner_product(scores, cot, ((0,), (0,))))
            moved = weighted * crossed[...]
            cumulative_cot[pl.ds(group * GROUP + i, 1), :] = jnp.sum(
                moved.T, axis=0, keepdims=True
            ) - jnp.sum(moved, axis=0, keepdims=True)
        crossed_cot[...] = total
        scaled_cot[:, group_lanes(group)] = jnp.concatenate(parts, axis=1)
        return carry

    lax.fori_loop(first, last, one, 0)
    if last == HEADS // GROUP:
        b_cot[...] = inner_product(crossed_cot[...], c_mat[...], ((0,), (0,)))
        c_cot[...] = inner_product(crossed_cot[...], b_mat[...], ((1,), (0,)))


def scan_kernel(count, reverse, work, inputs, outputs, *refs):
    state, decay = refs[:2]
    given = refs[2 : 2 + inputs]
    out = refs[2 + inputs]
    made = refs[3 + inputs : 3 + inputs + outputs]
    came, came_decay, ready = refs[3 + inputs + outputs : 6 + inputs + outputs]
    sems = refs[6 + inputs + outputs : 12 + inputs + outputs]
    held = refs[12 + inputs + outputs :]
    out_send, out_recv, decay_send, decay_recv, back_send, back_recv = sems
    dp_at, seq_at = places()
    barrier = pltpu.get_barrier_semaphore()
    peers = [(seq_at + hop) % count for hop in range(1, count)]
    for peer in peers:
        pl.semaphore_signal(barrier, inc=1, device_id=(dp_at, peer), device_id_type=MESH)
    pl.semaphore_wait(barrier, count - 1)

    def copy(hop, which):
        target = (seq_at + hop) % count
        source, landing, send_sem, recv_sem = (
            (state.at[target], came.at[seq_at], out_send, out_recv),
            (decay, came_decay.at[seq_at], decay_send, decay_recv),
            (ready.at[target], out.at[seq_at], back_send, back_recv),
        )[which]
        return pltpu.make_async_remote_copy(
            src_ref=source,
            dst_ref=landing,
            send_sem=send_sem.at[hop],
            recv_sem=recv_sem.at[hop],
            device_id=(dp_at, target),
            device_id_type=MESH,
        )

    for hop in range(1, count):
        copy(hop, 0).start()
        copy(hop, 1).start()
    came[seq_at] = state[seq_at]
    came_decay[seq_at] = decay[...]
    groups = HEADS // GROUP
    work(0, groups // 2, *given, *made, *held)
    for hop in range(1, count):
        copy(hop, 0).wait_recv()
        copy(hop, 1).wait_recv()
    total = jnp.zeros(state.shape[1:], jnp.float32)
    for place in range(count)[:: -1 if reverse else 1]:
        ready[place] = total.astype(ready.dtype)
        total = came_decay[place] * total + came[place].astype(jnp.float32)
    for hop in range(1, count):
        copy(hop, 2).start()
    out[seq_at] = ready[seq_at]
    work(groups // 2, groups, *given, *made, *held)
    for hop in range(1, count):
        copy(hop, 2).wait_recv()
    for hop in range(1, count):
        for which in range(3):
            copy(hop, which).wait_send()


def scan_states(state, decay, work, given, made, held, reverse, collective_id):
    count = lax.axis_size("seq")
    state = state.astype(jnp.bfloat16).reshape(count, STATE // count, DI)
    in_vmem = pl.BlockSpec(memory_space=pltpu.VMEM)
    got = pl.pallas_call(
        partial(scan_kernel, count, reverse, work, len(given), len(made)),
        out_shape=[jax.ShapeDtypeStruct(state.shape, state.dtype)]
        + [jax.ShapeDtypeStruct(shape, jnp.float32) for shape in made],
        in_specs=[in_vmem] * (2 + len(given)),
        out_specs=[in_vmem] * (1 + len(made)),
        scratch_shapes=[
            pltpu.VMEM(state.shape, state.dtype),
            pltpu.VMEM((count, 1, DI), jnp.float32),
            pltpu.VMEM(state.shape, state.dtype),
        ]
        + [pltpu.SemaphoreType.DMA((count,))] * 6
        + [pltpu.VMEM(shape, jnp.float32) for shape in held],
        compiler_params=pltpu.CompilerParams(
            collective_id=collective_id, has_side_effects=True, vmem_limit_bytes=VMEM_BYTES
        ),
        name="scan_back" if reverse else "scan_states",
    )(state, decay[None, :], *given)
    return got[0].reshape(STATE, DI).astype(jnp.float32), *got[1:]


def passed_along(value, axis, steps):
    count = lax.axis_size(axis)
    first, last = (max(0, -steps), min(count, count - steps))
    return lax.ppermute(value, axis, [(source, source + steps) for source in range(first, last)])


def pre_norm(residual_in, norm_gain):
    scale_rms = lax.rsqrt(jnp.mean(residual_in * residual_in, axis=-1, keepdims=True) + EPS)
    return residual_in * scale_rms * norm_gain


def conv_silu(padded, conv_weight, conv_bias, row_count):
    total = jnp.zeros((row_count, padded.shape[1]), jnp.float32) + conv_bias[None, :]
    for offset in range(conv_weight.shape[1]):
        total = total + conv_weight[:, offset][None, :] * padded[offset : offset + row_count]
    return jax.nn.silu(total)


def spread_heads(by_head):
    return jnp.repeat(by_head, HEAD_DIM, axis=-1)


def before_states(xbc, dt_raw, edge, conv_weight, conv_bias, dt_bias, a_log):
    row_count = xbc.shape[0]
    activated = conv_silu(jnp.concatenate([edge, xbc], axis=0), conv_weight, conv_bias, row_count)
    xs = activated[:, :DI]
    b_mat = activated[:, DI : DI + STATE]
    c_mat = activated[:, DI + STATE :]
    step = jax.nn.softplus(dt_raw + dt_bias)
    log_decay = step * -jnp.exp(a_log)
    at = jnp.arange(row_count)
    lower = (at[:, None] >= at[None, :]).astype(jnp.float32)
    cumulative = jnp.dot(lower, log_decay, precision=HIGH)
    scaled_x = xs * spread_heads(step)
    tail = jnp.exp(cumulative[-1][None, :] - cumulative)
    fresh = jnp.dot(b_mat.T, scaled_x * spread_heads(tail), precision=HIGH)
    return (xs, scaled_x, b_mat, c_mat, cumulative, fresh)


def post_gate(ssd_out, xs, gate_part, skip_gain, gated_gain):
    row_count = xs.shape[0]
    skipped = (xs.reshape(row_count, HEADS, HEAD_DIM) * skip_gain[None, :, None]).reshape(
        row_count, DI
    )
    mixed_in = (ssd_out + skipped) * jax.nn.silu(gate_part)
    scale_rms = lax.rsqrt(jnp.mean(mixed_in * mixed_in, axis=-1, keepdims=True) + EPS)
    return mixed_in * scale_rms * gated_gain


def contract_rows(left, right):
    return lax.dot_general(
        left, right, (((0,), (0,)), ((), ())), preferred_element_type=jnp.float32
    )


def contract_cols(left, right):
    return lax.dot_general(
        left, right, (((1,), (1,)), ((), ())), preferred_element_type=jnp.float32
    )


def body(
    inputs,
    norm_gain,
    in_proj,
    conv_weight,
    conv_bias,
    dt_bias,
    a_log,
    skip_gain,
    gated_gain,
    out_proj,
    cotangent,
):
    row_count = inputs.shape[0]
    residual_in = inputs.astype(jnp.float32)
    normed_full, norm_back = jax.vjp(pre_norm, residual_in, norm_gain)
    normed = normed_full.astype(jnp.bfloat16)
    in_whole, out_whole = gather_all(
        [jnp.pad(in_proj, ((0, 0), (0, WIDE - PROJ))), out_proj], collective_id=1
    )
    in_whole = in_whole.reshape(-1, WIDE)
    out_whole = out_whole.reshape(-1, DI)
    projected = jnp.dot(normed, in_whole, preferred_element_type=jnp.float32)
    gate_part = projected[:, :DI]
    xbc = projected[:, DI : DI + XBC]
    dt_raw = projected[:, DI + XBC : PROJ]
    edge = passed_along(xbc[row_count - (CONV - 1) :], "seq", 1)
    primal, mid_back = jax.vjp(
        before_states, xbc, dt_raw, edge, conv_weight, conv_bias, dt_bias, a_log
    )
    xs, scaled_x, b_mat, c_mat, cumulative, s_local = primal
    by_head = cumulative.T
    decay = jnp.exp(cumulative[-1])
    wide_decay = spread_heads(decay)
    square = (row_count, row_count)
    state_in, local_out = scan_states(
        s_local,
        wide_decay,
        inside_work,
        [scaled_x, b_mat, c_mat, by_head],
        [xs.shape],
        [square],
        False,
        collective_id=2,
    )
    weighted = spread_heads(jnp.exp(cumulative))
    carried_part = jnp.dot(c_mat, state_in, precision=HIGH) * weighted
    ssd_out = local_out + carried_part
    gated_full, post_back = jax.vjp(post_gate, ssd_out, xs, gate_part, skip_gain, gated_gain)
    gated = gated_full.astype(jnp.bfloat16)
    mixed = contract_cols(gated, out_whole)
    layer_out = (residual_in + mixed).astype(jnp.bfloat16)
    gated_cot = jnp.dot(cotangent, out_whole, preferred_element_type=jnp.float32)
    ssd_cot, xs_cot, gate_cot, skip_grad, gated_gain_grad = post_back(gated_cot)
    scaled_cot = ssd_cot * weighted
    local_grad = jnp.dot(c_mat.T, scaled_cot, precision=HIGH)
    later_grad, scaled_x_cot, b_cot, inner_c_cot, by_head_cot = scan_states(
        local_grad,
        wide_decay,
        inside_back,
        [ssd_cot, scaled_x, b_mat, c_mat, by_head],
        [xs.shape, b_mat.shape, c_mat.shape, by_head.shape],
        [square, square],
        True,
        collective_id=3,
    )
    c_cot = lax.dot_general(scaled_cot, state_in, (((1,), (1,)), ((), ())), precision=HIGH)
    cum_cot = jnp.sum((ssd_cot * carried_part).reshape(row_count, HEADS, HEAD_DIM), axis=2)
    last_cot = jnp.sum(later_grad * state_in, axis=0).reshape(HEADS, HEAD_DIM).sum(axis=1) * decay
    is_last = (jnp.arange(row_count) == row_count - 1)[:, None]
    cum_cot = cum_cot + jnp.where(is_last, last_cot[None, :], 0.0)
    mid_grads = mid_back(
        (xs_cot, scaled_x_cot, b_cot, c_cot + inner_c_cot, cum_cot + by_head_cot.T, later_grad)
    )
    xbc_cot, dt_cot, edge_cot, conv_weight_grad, conv_bias_grad, dt_bias_grad, a_log_grad = (
        mid_grads
    )
    edge_back = passed_along(edge_cot, "seq", -1)
    xbc_cot = xbc_cot + jnp.pad(edge_back, ((row_count - (CONV - 1), 0), (0, 0)))
    projected_cot = jnp.concatenate(
        [gate_cot, xbc_cot, dt_cot, jnp.zeros((row_count, WIDE - PROJ), jnp.float32)], axis=1
    ).astype(jnp.bfloat16)
    in_term = contract_rows(normed, projected_cot).astype(jnp.bfloat16)
    out_term = contract_rows(cotangent, gated).astype(jnp.bfloat16)
    normed_cot = contract_cols(projected_cot, in_whole)
    input_part, norm_gain_grad = norm_back(normed_cot)
    input_grad = cotangent.astype(jnp.float32) + input_part
    small = (
        norm_gain_grad,
        conv_weight_grad.T,
        conv_bias_grad,
        gated_gain_grad,
        dt_bias_grad,
        a_log_grad,
        skip_grad,
    )
    flat = jnp.concatenate([a.reshape(-1) for a in small])
    tile = 8 * LANES
    flat = jnp.pad(flat, (0, -flat.shape[0] % tile))
    in_proj_grad, out_proj_grad, summed = sum_to_owners(
        [in_term, out_term], flat.reshape(-1, LANES), collective_id=4
    )
    summed = summed.reshape(-1)
    parts, at = [], 0
    for a in small:
        parts.append(summed[at : at + a.size].reshape(a.shape))
        at += a.size
    return (
        layer_out,
        input_grad,
        in_proj_grad[:, :PROJ],
        out_proj_grad,
        parts[0],
        parts[1].T,
        parts[2],
        parts[4],
        parts[5],
        parts[6],
        parts[3],
    )


def solution(mesh):
    placed = (
        P(("dp", "seq"), None),
        P(),
        P(("dp", "seq"), None),
        P(),
        P(),
        P(),
        P(),
        P(),
        P(),
        P(("dp", "seq"), None),
        P(("dp", "seq"), None),
    )
    return jax.shard_map(
        body,
        mesh=mesh,
        in_specs=placed,
        out_specs=(
            P(("dp", "seq"), None),
            P(("dp", "seq"), None),
            P(("dp", "seq"), None),
            P(("dp", "seq"), None),
            P(),
            P(),
            P(),
            P(),
            P(),
            P(),
            P(),
        ),
        check_vma=False,
    )
```

```python
from functools import partial

import jax
import jax.numpy as jnp
from jax import lax
from jax.experimental import pallas as pl
from jax.experimental.pallas import tpu as pltpu
from jax.sharding import PartitionSpec as P

HEADS = 24
HEAD_DIM = 64
STATE = 128
CONV = 4
DI = 1536
XBC = 1792
PROJ = DI + XBC + HEADS
LANES = 128
WIDE = -(-PROJ // LANES) * LANES


EPS = 1e-05
HIGH = lax.Precision.HIGHEST
MESH = pl.DeviceIdType.MESH
VMEM_BYTES = 60 * 1024 * 1024


def bits_of(count):
    return count.bit_length() - 1


def bit_at(place, bit):
    return (place // 2**bit) % 2


def places():
    return lax.axis_index("dp"), lax.axis_index("seq")


def partner(bit, seq_bits):
    dp_at, seq_at = places()
    if bit < seq_bits:
        return dp_at, seq_at + (1 - 2 * bit_at(seq_at, bit)) * 2**bit
    up = bit - seq_bits
    return dp_at + (1 - 2 * bit_at(dp_at, up)) * 2**up, seq_at


def greet(bits, seq_bits):
    barrier = pltpu.get_barrier_semaphore()
    for bit in range(bits):
        pl.semaphore_signal(barrier, inc=1, device_id=partner(bit, seq_bits), device_id_type=MESH)
    pl.semaphore_wait(barrier, bits)


def gather_orders(seq_bits, dp_bits):
    x_count = seq_bits // 2
    x_bits = list(range(x_count))
    z_bits = list(range(x_count, seq_bits))[::-1]
    core = [seq_bits]
    y_bits = [seq_bits + 1 + i for i in range(dp_bits - 1)]
    return (
        z_bits + x_bits + y_bits + core,
        z_bits + y_bits + x_bits + core,
        z_bits[:1] + x_bits + y_bits + z_bits[1:] + core,
        z_bits[:1] + y_bits + x_bits + z_bits[1:] + core,
    )


SHARES = (0.3, 0.3, 0.2, 0.2)


def split_lanes(width, shares):
    tiles = width // LANES
    edges = [round(tiles * sum(shares[:i])) * LANES for i in range(len(shares) + 1)]
    return [(low, high - low) for low, high in zip(edges, edges[1:])]


def gather_kernel(seq_bits, streams, bits, *refs):
    array_count = 1 + max(stream[0] for stream in streams)
    shards, outs = refs[:array_count], refs[array_count : 2 * array_count]
    send_sem, recv_sem, own_sem = refs[2 * array_count :]
    dp_at, seq_at = places()
    place = dp_at * 2**seq_bits + seq_at
    own = [
        pltpu.make_async_copy(shard, out.at[place], own_sem.at[i])
        for i, (shard, out) in enumerate(zip(shards, outs))
    ]
    for copy in own:
        copy.start()
    greet(bits, seq_bits)
    for copy in own:
        copy.wait()

    def landed(stream, stage, sem):
        which, low, width, _ = streams[stream]
        view = outs[which].at[pl.ds(0, 2**stage), :, pl.ds(low, width)]
        pltpu.make_async_copy(view, view, sem.at[stream, stage]).wait()

    for stage in range(bits + 1):
        for stream, (which, low, width, order) in enumerate(streams):
            if stage > 0:
                landed(stream, stage - 1, recv_sem)
            if stage == bits:
                continue
            free = order[:stage]
            run = 0
            while run in free:
                run += 1
            base = place
            for bit in free:
                base = base - bit_at(place, bit) * 2**bit
            upper = [bit for bit in free if bit > run]
            for combo in range(2 ** len(upper)):
                start = base + sum(2**bit for i, bit in enumerate(upper) if combo >> i & 1)
                view = outs[which].at[pl.ds(start, 2**run), :, pl.ds(low, width)]
                pltpu.make_async_remote_copy(
                    src_ref=view,
                    dst_ref=view,
                    send_sem=send_sem.at[stream, stage],
                    recv_sem=recv_sem.at[stream, stage],
                    device_id=partner(order[stage], seq_bits),
                    device_id_type=MESH,
                ).start()
    for stage in range(bits):
        for stream in range(len(streams)):
            landed(stream, stage, send_sem)


def gather_all(shards, collective_id):
    seq_bits, dp_bits = bits_of(lax.axis_size("seq")), bits_of(lax.axis_size("dp"))
    bits = seq_bits + dp_bits
    orders = gather_orders(seq_bits, dp_bits)
    streams = [
        (which, low, width, order)
        for which, shard in enumerate(shards)
        for (low, width), order in zip(split_lanes(shard.shape[1], SHARES), orders)
    ]
    return pl.pallas_call(
        partial(gather_kernel, seq_bits, streams, bits),
        out_shape=[jax.ShapeDtypeStruct((2**bits, *a.shape), a.dtype) for a in shards],
        in_specs=[pl.BlockSpec(memory_space=pltpu.VMEM)] * len(shards),
        out_specs=[pl.BlockSpec(memory_space=pl.ANY)] * len(shards),
        scratch_shapes=[
            pltpu.SemaphoreType.DMA((len(streams), bits)),
            pltpu.SemaphoreType.DMA((len(streams), bits)),
            pltpu.SemaphoreType.DMA((len(shards),)),
        ],
        compiler_params=pltpu.CompilerParams(
            collective_id=collective_id, has_side_effects=True, vmem_limit_bytes=VMEM_BYTES
        ),
        name="gather_rows",
    )(*shards)


def sum_kernel(seq_bits, streams, bits, array_count, *refs):
    terms, vector = refs[:array_count], refs[array_count]
    outs, vector_out = refs[array_count + 1 : 2 * array_count + 1], refs[2 * array_count + 1]
    held = refs[2 * array_count + 2 : 2 * array_count + 2 + len(streams) * bits]
    rest = refs[2 * array_count + 2 + len(streams) * bits :]
    vector_in, vector_sum, send_sem, recv_sem, vector_send, vector_recv = rest
    dp_at, seq_at = places()
    place = dp_at * 2**seq_bits + seq_at
    greet(bits, seq_bits)

    def source(stream, stage):
        which, low, width, _ = streams[stream]
        if stage == 0:
            return terms[which], pl.ds(low, width)
        return held[stream * bits + stage - 1], pl.ds(0, width)

    def position(stream, stage):
        order = streams[stream][3]
        remaining = sorted(order[stage:])
        return remaining.index(order[stage]), bit_at(place, order[stage])

    def landed(stream, stage, sem):
        view = held[stream * bits + stage]
        pltpu.make_async_copy(view, view, sem.at[stream, stage]).wait()

    def vector_copy(stage):
        return pltpu.make_async_remote_copy(
            src_ref=vector if stage == 0 else vector_sum.at[stage - 1],
            dst_ref=vector_in.at[stage],
            send_sem=vector_send.at[stage],
            recv_sem=vector_recv.at[stage],
            device_id=partner(stage, seq_bits),
            device_id_type=MESH,
        )

    for stage in range(bits + 1):
        if stage > 0:
            vector_copy(stage - 1).wait_recv()
            before = vector[...] if stage == 1 else vector_sum[stage - 2]
            total = before + vector_in[stage - 1]
            if stage < bits:
                vector_sum[stage - 1] = total
            else:
                vector_out[...] = total
        if stage < bits:
            vector_copy(stage).start()
        for stream, (which, low, width, order) in enumerate(streams):
            if stage > 0:
                landed(stream, stage - 1, recv_sem)
                spot, mine = position(stream, stage - 1)
                kept, lanes = source(stream, stage - 1)
                came = held[stream * bits + stage - 1]
                if stage == bits:
                    outs[which][:, pl.ds(low, width)] = kept[mine, :, lanes].astype(
                        jnp.float32
                    ) + came[0].astype(jnp.float32)
                    continue

                def add_one(block, carry, spot=spot, mine=mine, kept=kept, lanes=lanes, came=came):
                    from_block = (block // 2**spot) * 2 ** (spot + 1) + mine * 2**spot
                    from_block = from_block + block % 2**spot
                    added = kept[from_block, :, lanes].astype(jnp.float32) + came[block].astype(
                        jnp.float32
                    )
                    came[block] = added.astype(came.dtype)
                    return carry

                lax.fori_loop(0, 2 ** (bits - stage), add_one, 0)
            spot, mine = position(stream, stage)
            sent, lanes = source(stream, stage)
            for high in range(2 ** (bits - stage - 1 - spot)):
                start = high * 2 ** (spot + 1) + (1 - mine) * 2**spot
                pltpu.make_async_remote_copy(
                    src_ref=sent.at[pl.ds(start, 2**spot), :, lanes],
                    dst_ref=held[stream * bits + stage].at[pl.ds(high * 2**spot, 2**spot)],
                    send_sem=send_sem.at[stream, stage],
                    recv_sem=recv_sem.at[stream, stage],
                    device_id=partner(order[stage], seq_bits),
                    device_id_type=MESH,
                ).start()
    for stage in range(bits):
        vector_copy(stage).wait_send()
        for stream in range(len(streams)):
            landed(stream, stage, send_sem)


def sum_to_owners(terms, vector, collective_id):
    seq_bits, dp_bits = bits_of(lax.axis_size("seq")), bits_of(lax.axis_size("dp"))
    bits = seq_bits + dp_bits
    orders = [order[::-1] for order in gather_orders(seq_bits, dp_bits)]
    terms = [term.reshape(2**bits, -1, term.shape[1]) for term in terms]
    streams = [
        (which, low, width, order)
        for which, term in enumerate(terms)
        for (low, width), order in zip(split_lanes(term.shape[2], SHARES), orders)
    ]
    rows = terms[0].shape[1]
    in_vmem = pl.BlockSpec(memory_space=pltpu.VMEM)
    held = [
        pltpu.VMEM((2 ** (bits - 1 - stage), rows, width), jnp.bfloat16)
        for _, _, width, _ in streams
        for stage in range(bits)
    ]
    return pl.pallas_call(
        partial(sum_kernel, seq_bits, streams, bits, len(terms)),
        out_shape=[jax.ShapeDtypeStruct(a.shape[1:], jnp.float32) for a in terms]
        + [jax.ShapeDtypeStruct(vector.shape, vector.dtype)],
        in_specs=[in_vmem] * (len(terms) + 1),
        out_specs=[in_vmem] * (len(terms) + 1),
        scratch_shapes=held
        + [
            pltpu.VMEM((bits, *vector.shape), jnp.float32),
            pltpu.VMEM((bits, *vector.shape), jnp.float32),
            pltpu.SemaphoreType.DMA((len(streams), bits)),
            pltpu.SemaphoreType.DMA((len(streams), bits)),
            pltpu.SemaphoreType.DMA((bits,)),
            pltpu.SemaphoreType.DMA((bits,)),
        ],
        compiler_params=pltpu.CompilerParams(
            collective_id=collective_id, has_side_effects=True, vmem_limit_bytes=VMEM_BYTES
        ),
        name="sum_rows",
    )(*terms, vector)


GROUP = 4
GROUP_LANES = GROUP * HEAD_DIM


def inner_product(left, right, dims):
    return lax.dot_general(
        left, right, (dims, ((), ())), precision=HIGH, preferred_element_type=jnp.float32
    )


def group_lanes(group):
    return pl.ds(pl.multiple_of(group * GROUP_LANES, GROUP_LANES), GROUP_LANES)


def head_weights(cumulative, head):
    row = cumulative[pl.ds(head, 1), :]
    count = row.shape[1]
    spread = jnp.broadcast_to(row, (count, count))
    later = lax.broadcasted_iota(jnp.int32, (count, count), 0)
    earlier = lax.broadcasted_iota(jnp.int32, (count, count), 1)
    return jnp.exp(jnp.where(later >= earlier, spread.T - spread, -jnp.inf))


def inside_work(first, last, scaled_x, b_mat, c_mat, cumulative, output, crossed):
    if first == 0:
        crossed[...] = inner_product(c_mat[...], b_mat[...], ((1,), (1,)))

    def one(group, carry):
        values = scaled_x[:, group_lanes(group)]
        parts = []
        for i in range(GROUP):
            scores = head_weights(cumulative, group * GROUP + i) * crossed[...]
            head = values[:, i * HEAD_DIM : (i + 1) * HEAD_DIM]
            parts.append(inner_product(scores, head, ((1,), (0,))))
        output[:, group_lanes(group)] = jnp.concatenate(parts, axis=1)
        return carry

    lax.fori_loop(first, last, one, 0)


def inside_back(
    first,
    last,
    output_cot,
    scaled_x,
    b_mat,
    c_mat,
    cumulative,
    scaled_cot,
    b_cot,
    c_cot,
    cumulative_cot,
    crossed,
    crossed_cot,
):
    if first == 0:
        crossed[...] = inner_product(c_mat[...], b_mat[...], ((1,), (1,)))
        crossed_cot[...] = jnp.zeros_like(crossed_cot)

    def one(group, carry):
        values = scaled_x[:, group_lanes(group)]
        cots = output_cot[:, group_lanes(group)]
        parts = []
        total = crossed_cot[...]
        for i in range(GROUP):
            weights = head_weights(cumulative, group * GROUP + i)
            scores = weights * crossed[...]
            head = values[:, i * HEAD_DIM : (i + 1) * HEAD_DIM]
            cot = cots[:, i * HEAD_DIM : (i + 1) * HEAD_DIM]
            weighted = weights * inner_product(cot, head, ((1,), (1,)))
            total = total + weighted
            parts.append(inner_product(scores, cot, ((0,), (0,))))
            moved = weighted * crossed[...]
            cumulative_cot[pl.ds(group * GROUP + i, 1), :] = jnp.sum(
                moved.T, axis=0, keepdims=True
            ) - jnp.sum(moved, axis=0, keepdims=True)
        crossed_cot[...] = total
        scaled_cot[:, group_lanes(group)] = jnp.concatenate(parts, axis=1)
        return carry

    lax.fori_loop(first, last, one, 0)
    if last == HEADS // GROUP:
        b_cot[...] = inner_product(crossed_cot[...], c_mat[...], ((0,), (0,)))
        c_cot[...] = inner_product(crossed_cot[...], b_mat[...], ((1,), (0,)))


def scan_kernel(count, reverse, work, inputs, outputs, *refs):
    state, decay = refs[:2]
    given = refs[2 : 2 + inputs]
    out = refs[2 + inputs]
    made = refs[3 + inputs : 3 + inputs + outputs]
    came, came_decay, ready = refs[3 + inputs + outputs : 6 + inputs + outputs]
    sems = refs[6 + inputs + outputs : 12 + inputs + outputs]
    held = refs[12 + inputs + outputs :]
    out_send, out_recv, decay_send, decay_recv, back_send, back_recv = sems
    dp_at, seq_at = places()
    barrier = pltpu.get_barrier_semaphore()
    peers = [(seq_at + hop) % count for hop in range(1, count)]
    for peer in peers:
        pl.semaphore_signal(barrier, inc=1, device_id=(dp_at, peer), device_id_type=MESH)
    pl.semaphore_wait(barrier, count - 1)

    def copy(hop, which):
        target = (seq_at + hop) % count
        source, landing, send_sem, recv_sem = (
            (state.at[target], came.at[seq_at], out_send, out_recv),
            (decay, came_decay.at[seq_at], decay_send, decay_recv),
            (ready.at[target], out.at[seq_at], back_send, back_recv),
        )[which]
        return pltpu.make_async_remote_copy(
            src_ref=source,
            dst_ref=landing,
            send_sem=send_sem.at[hop],
            recv_sem=recv_sem.at[hop],
            device_id=(dp_at, target),
            device_id_type=MESH,
        )

    for hop in range(1, count):
        copy(hop, 0).start()
        copy(hop, 1).start()
    came[seq_at] = state[seq_at]
    came_decay[seq_at] = decay[...]
    groups = HEADS // GROUP
    work(0, groups // 2, *given, *made, *held)
    for hop in range(1, count):
        copy(hop, 0).wait_recv()
        copy(hop, 1).wait_recv()
    total = jnp.zeros(state.shape[1:], jnp.float32)
    for place in range(count)[:: -1 if reverse else 1]:
        ready[place] = total.astype(ready.dtype)
        total = came_decay[place] * total + came[place].astype(jnp.float32)
    for hop in range(1, count):
        copy(hop, 2).start()
    out[seq_at] = ready[seq_at]
    work(groups // 2, groups, *given, *made, *held)
    for hop in range(1, count):
        copy(hop, 2).wait_recv()
    for hop in range(1, count):
        for which in range(3):
            copy(hop, which).wait_send()


def scan_states(state, decay, work, given, made, held, reverse, collective_id):
    count = lax.axis_size("seq")
    state = state.astype(jnp.bfloat16).reshape(count, STATE // count, DI)
    in_vmem = pl.BlockSpec(memory_space=pltpu.VMEM)
    got = pl.pallas_call(
        partial(scan_kernel, count, reverse, work, len(given), len(made)),
        out_shape=[jax.ShapeDtypeStruct(state.shape, state.dtype)]
        + [jax.ShapeDtypeStruct(shape, jnp.float32) for shape in made],
        in_specs=[in_vmem] * (2 + len(given)),
        out_specs=[in_vmem] * (1 + len(made)),
        scratch_shapes=[
            pltpu.VMEM(state.shape, state.dtype),
            pltpu.VMEM((count, 1, DI), jnp.float32),
            pltpu.VMEM(state.shape, state.dtype),
        ]
        + [pltpu.SemaphoreType.DMA((count,))] * 6
        + [pltpu.VMEM(shape, jnp.float32) for shape in held],
        compiler_params=pltpu.CompilerParams(
            collective_id=collective_id, has_side_effects=True, vmem_limit_bytes=VMEM_BYTES
        ),
        name="scan_back" if reverse else "scan_states",
    )(state, decay[None, :], *given)
    return got[0].reshape(STATE, DI).astype(jnp.float32), *got[1:]


def passed_along(value, axis, steps):
    count = lax.axis_size(axis)
    first, last = (max(0, -steps), min(count, count - steps))
    return lax.ppermute(value, axis, [(source, source + steps) for source in range(first, last)])


def pre_norm(residual_in, norm_gain):
    scale_rms = lax.rsqrt(jnp.mean(residual_in * residual_in, axis=-1, keepdims=True) + EPS)
    return residual_in * scale_rms * norm_gain


def conv_silu(padded, conv_weight, conv_bias, row_count):
    total = jnp.zeros((row_count, padded.shape[1]), jnp.float32) + conv_bias[None, :]
    for offset in range(conv_weight.shape[1]):
        total = total + conv_weight[:, offset][None, :] * padded[offset : offset + row_count]
    return jax.nn.silu(total)


def head_lanes():
    lanes = jnp.arange(DI, dtype=jnp.int32) // HEAD_DIM
    return (jnp.arange(HEADS, dtype=jnp.int32)[:, None] == lanes[None, :]).astype(jnp.float32)


def spread_heads(by_head):
    return jnp.dot(by_head, head_lanes(), precision=HIGH)


def sum_heads(by_lane):
    return jnp.dot(by_lane, head_lanes().T, precision=HIGH)


def before_states(xbc, dt_raw, edge, conv_weight, conv_bias, dt_bias, a_log):
    row_count = xbc.shape[0]
    activated = conv_silu(jnp.concatenate([edge, xbc], axis=0), conv_weight, conv_bias, row_count)
    xs = activated[:, :DI]
    b_mat = activated[:, DI : DI + STATE]
    c_mat = activated[:, DI + STATE :]
    step = jax.nn.softplus(dt_raw + dt_bias)
    log_decay = step * -jnp.exp(a_log)
    at = jnp.arange(row_count)
    lower = (at[:, None] >= at[None, :]).astype(jnp.float32)
    cumulative = jnp.dot(lower, log_decay, precision=HIGH)
    scaled_x = xs * spread_heads(step)
    tail = jnp.exp(cumulative[-1][None, :] - cumulative)
    fresh = jnp.dot(b_mat.T, scaled_x * spread_heads(tail), precision=HIGH)
    return (xs, scaled_x, b_mat, c_mat, cumulative, fresh)


def post_gate(ssd_out, xs, gate_part, skip_gain, gated_gain):
    skipped = xs * spread_heads(skip_gain[None, :])
    mixed_in = (ssd_out + skipped) * jax.nn.silu(gate_part)
    scale_rms = lax.rsqrt(jnp.mean(mixed_in * mixed_in, axis=-1, keepdims=True) + EPS)
    return mixed_in * scale_rms * gated_gain


def contract_rows(left, right):
    return lax.dot_general(
        left, right, (((0,), (0,)), ((), ())), preferred_element_type=jnp.float32
    )


def contract_cols(left, right):
    return lax.dot_general(
        left, right, (((1,), (1,)), ((), ())), preferred_element_type=jnp.float32
    )


def body(
    inputs,
    norm_gain,
    in_proj,
    conv_weight,
    conv_bias,
    dt_bias,
    a_log,
    skip_gain,
    gated_gain,
    out_proj,
    cotangent,
):
    row_count = inputs.shape[0]
    residual_in = inputs.astype(jnp.float32)
    normed_full, norm_back = jax.vjp(pre_norm, residual_in, norm_gain)
    normed = normed_full.astype(jnp.bfloat16)
    in_whole, out_whole = gather_all(
        [jnp.pad(in_proj, ((0, 0), (0, WIDE - PROJ))), out_proj], collective_id=1
    )
    in_whole = in_whole.reshape(-1, WIDE)
    out_whole = out_whole.reshape(-1, DI)
    projected = jnp.dot(normed, in_whole, preferred_element_type=jnp.float32)
    gate_part = projected[:, :DI]
    xbc = projected[:, DI : DI + XBC]
    dt_raw = projected[:, DI + XBC : PROJ]
    edge = passed_along(xbc[row_count - (CONV - 1) :], "seq", 1)
    primal, mid_back = jax.vjp(
        before_states, xbc, dt_raw, edge, conv_weight, conv_bias, dt_bias, a_log
    )
    xs, scaled_x, b_mat, c_mat, cumulative, s_local = primal
    by_head = cumulative.T
    decay = jnp.exp(cumulative[-1])
    wide_decay = spread_heads(decay[None, :])[0]
    square = (row_count, row_count)
    state_in, local_out = scan_states(
        s_local,
        wide_decay,
        inside_work,
        [scaled_x, b_mat, c_mat, by_head],
        [xs.shape],
        [square],
        False,
        collective_id=2,
    )
    weighted = spread_heads(jnp.exp(cumulative))
    carried_part = jnp.dot(c_mat, state_in, precision=HIGH) * weighted
    ssd_out = local_out + carried_part
    gated_full, post_back = jax.vjp(post_gate, ssd_out, xs, gate_part, skip_gain, gated_gain)
    gated = gated_full.astype(jnp.bfloat16)
    mixed = contract_cols(gated, out_whole)
    layer_out = (residual_in + mixed).astype(jnp.bfloat16)
    gated_cot = jnp.dot(cotangent, out_whole, preferred_element_type=jnp.float32)
    ssd_cot, xs_cot, gate_cot, skip_grad, gated_gain_grad = post_back(gated_cot)
    scaled_cot = ssd_cot * weighted
    local_grad = jnp.dot(c_mat.T, scaled_cot, precision=HIGH)
    later_grad, scaled_x_cot, b_cot, inner_c_cot, by_head_cot = scan_states(
        local_grad,
        wide_decay,
        inside_back,
        [ssd_cot, scaled_x, b_mat, c_mat, by_head],
        [xs.shape, b_mat.shape, c_mat.shape, by_head.shape],
        [square, square],
        True,
        collective_id=3,
    )
    c_cot = lax.dot_general(scaled_cot, state_in, (((1,), (1,)), ((), ())), precision=HIGH)
    cum_cot = sum_heads(ssd_cot * carried_part)
    last_cot = sum_heads(jnp.sum(later_grad * state_in, axis=0, keepdims=True))[0] * decay
    is_last = (jnp.arange(row_count) == row_count - 1)[:, None]
    cum_cot = cum_cot + jnp.where(is_last, last_cot[None, :], 0.0)
    mid_grads = mid_back(
        (xs_cot, scaled_x_cot, b_cot, c_cot + inner_c_cot, cum_cot + by_head_cot.T, later_grad)
    )
    xbc_cot, dt_cot, edge_cot, conv_weight_grad, conv_bias_grad, dt_bias_grad, a_log_grad = (
        mid_grads
    )
    edge_back = passed_along(edge_cot, "seq", -1)
    xbc_cot = xbc_cot + jnp.pad(edge_back, ((row_count - (CONV - 1), 0), (0, 0)))
    projected_cot = jnp.concatenate(
        [gate_cot, xbc_cot, dt_cot, jnp.zeros((row_count, WIDE - PROJ), jnp.float32)], axis=1
    ).astype(jnp.bfloat16)
    in_term = contract_rows(normed, projected_cot).astype(jnp.bfloat16)
    out_term = contract_rows(cotangent, gated).astype(jnp.bfloat16)
    normed_cot = contract_cols(projected_cot, in_whole)
    input_part, norm_gain_grad = norm_back(normed_cot)
    input_grad = cotangent.astype(jnp.float32) + input_part
    small = (
        norm_gain_grad,
        conv_weight_grad.T,
        conv_bias_grad,
        gated_gain_grad,
        dt_bias_grad,
        a_log_grad,
        skip_grad,
    )
    flat = jnp.concatenate([a.reshape(-1) for a in small])
    tile = 8 * LANES
    flat = jnp.pad(flat, (0, -flat.shape[0] % tile))
    in_proj_grad, out_proj_grad, summed = sum_to_owners(
        [in_term, out_term], flat.reshape(-1, LANES), collective_id=4
    )
    summed = summed.reshape(-1)
    parts, at = [], 0
    for a in small:
        parts.append(summed[at : at + a.size].reshape(a.shape))
        at += a.size
    return (
        layer_out,
        input_grad,
        in_proj_grad[:, :PROJ],
        out_proj_grad,
        parts[0],
        parts[1].T,
        parts[2],
        parts[4],
        parts[5],
        parts[6],
        parts[3],
    )


def solution(mesh):
    placed = (
        P(("dp", "seq"), None),
        P(),
        P(("dp", "seq"), None),
        P(),
        P(),
        P(),
        P(),
        P(),
        P(),
        P(("dp", "seq"), None),
        P(("dp", "seq"), None),
    )
    return jax.shard_map(
        body,
        mesh=mesh,
        in_specs=placed,
        out_specs=(
            P(("dp", "seq"), None),
            P(("dp", "seq"), None),
            P(("dp", "seq"), None),
            P(("dp", "seq"), None),
            P(),
            P(),
            P(),
            P(),
            P(),
            P(),
            P(),
        ),
        check_vma=False,
    )
```
